32 devices in a mesh: loop: 16 (over z, x, core), team: 2 (over y).
Axes of the slice: x: 2, y: 2, z: 4, core: 2. Of those that a mesh axis runs over, the one named last changes fastest.
Arguments:
- blocks: bfloat16 [4096, 128, 128], P(('loop', 'team')), may hold values from -0.078125 to 0.078125
- probes: bfloat16 [32768, 128], P(('loop', 'team')), may hold values from -6 to 6
- row_count: int32 [64], P(('loop', 'team')), may hold values from 0 to 64, as said below
- column_of_slot: int32 [4096], P(('loop', 'team')), may hold values from 0 to 255, as said below
Outputs:
- sketch: float32 [8192, 128], P(('loop', 'team'))
The draws below stay inside these ranges and needn't reach their ends.
Inputs may be any that keep to these rules, and one draw needn't show every extreme that they name: `row_count`: A device's block rows hold 128 stored blocks or fewer together, and some device holds exactly 128; each block row holds at most min(64, 128), some block row exactly that many, and some block row none. `column_of_slot`: A used slot of a device in loop position t holds a block column in the pieces of loop indices t, t-1, ..., t-3 (mod 16), piece p covering block columns p * 16 to p * 16 + 15; columns within one block row are distinct. Unused slots hold columns of the same range.
All inputs are finite; a program needn't handle non-finite values.
Results may differ from the reference program's by a relative error of at most 0.0003.
Values may be sent and summed in bfloat16 or wider, within the bound.
A program may use at most 64 MiB of HBM per device.

```python
import jax
import jax.numpy as jnp
from jax import lax

BLOCK_EDGE = 128
PROBES = 128
CB = 16
RB = 2
DEVICE_SLOTS = 128
BLOCK_REACH = 64
CELLS = 32768
ROWS = 8192
TOTAL_SLOTS = 4096
N_LOOP = 16
DEVICES = 32


def pattern_helper(key):
    base = jax.random.fold_in(key, 7)
    key_overall = jax.random.fold_in(base, 1)
    key_full = jax.random.fold_in(base, 2)
    key_perm = jax.random.fold_in(base, 3)
    key_split = jax.random.fold_in(base, 4)
    device_numbers = jnp.arange(DEVICES, dtype=jnp.int32)
    running_sums = jax.random.randint(key_overall, (DEVICES,), DEVICE_SLOTS // 4, DEVICE_SLOTS + 1).astype(jnp.int32)
    device_filled = jax.random.randint(key_full, (), 0, DEVICES).astype(jnp.int32)
    empty_device = ((device_filled + 1) % DEVICES).astype(jnp.int32)
    running_sums = jnp.where(device_numbers == device_filled, DEVICE_SLOTS, running_sums)
    running_sums = jnp.where(device_numbers == empty_device, jnp.minimum(running_sums, BLOCK_REACH), running_sums).astype(jnp.int32)
    remain = running_sums
    count_list = []
    for row_number in range(RB - 1):
        rest_cap = (RB - 1 - row_number) * BLOCK_REACH
        low = jnp.maximum(0, remain - rest_cap)
        high = jnp.minimum(BLOCK_REACH, remain)
        part_key = jax.random.fold_in(key_split, row_number)
        selected_rows = jax.random.randint(part_key, (DEVICES,), low, high + 1).astype(jnp.int32)
        if row_number == 0:
            selected_rows = jnp.where(device_numbers == device_filled, min(BLOCK_REACH, DEVICE_SLOTS), selected_rows)
            selected_rows = jnp.where(device_numbers == empty_device, 0, selected_rows).astype(jnp.int32)
        count_list.append(selected_rows)
        remain = remain - selected_rows
    count_list.append(remain)
    counts = jnp.stack(count_list, axis=1).astype(jnp.int32)
    ends = jnp.cumsum(counts, axis=1).astype(jnp.int32)
    starts = (ends - counts).astype(jnp.int32)
    slot_entries = jnp.arange(DEVICE_SLOTS, dtype=jnp.int32)
    owner = jnp.sum((slot_entries[None, :, None] >= ends[:, None, :]).astype(jnp.int32), axis=2)
    owner_row = jnp.minimum(owner, RB - 1)
    start_of = jnp.take_along_axis(starts, owner_row, axis=1)
    rank = jnp.where(owner < RB, slot_entries[None, :] - start_of, slot_entries[None, :]) % BLOCK_REACH
    perm_keys = jax.random.split(key_perm, DEVICES * RB)
    perms = jax.vmap(lambda one_key: jax.random.permutation(one_key, BLOCK_REACH))(perm_keys)
    perms = perms.reshape(DEVICES, RB, BLOCK_REACH).astype(jnp.int32)
    flat_index = owner_row * BLOCK_REACH + rank
    position = jnp.take_along_axis(perms.reshape(DEVICES, RB * BLOCK_REACH), flat_index, axis=1)
    stop = position // CB
    within = position % CB
    team_count = DEVICES // N_LOOP
    loop_of = (device_numbers // team_count)[:, None]
    piece = (loop_of - stop) % N_LOOP
    column = (piece * CB + within).astype(jnp.int32)
    return (counts.reshape(-1), column.reshape(-1))


def draw_row_count(key, part):
    return pattern_helper(key)[0]


def draw_column_of_slot(key, part):
    return pattern_helper(key)[1]


def steps_of(own_key, dims, shards, low, largest):
    def one(dim, blocks):
        steps = jax.random.uniform(jax.random.fold_in(jax.random.fold_in(own_key, 6), dim), (blocks,), jnp.float32, low / len(shards), largest / len(shards))
        return jnp.repeat(jnp.exp(steps), dims[dim] // blocks).reshape((-1,) + (1,) * (len(dims) - dim - 1))

    loudness = one(*shards[0])
    for cut in shards[1:]:
        loudness = loudness * one(*cut)
    return loudness


def scatter_about(own_key, shape, width, most, cuts=(), held_as=jnp.bfloat16):
    gain = steps_of(own_key, shape, cuts, -0.22, 0.18) if cuts else 1.0
    array = jax.random.normal(own_key, shape, jnp.float32) * width * gain
    return jnp.minimum(jnp.maximum(array, -most), most).astype(held_as)


def setup_inputs(seed: int = 0) -> dict:
    keys = jax.random.split(jax.random.key(seed), 5)
    return {
        "blocks": scatter_about(keys[0], (TOTAL_SLOTS, BLOCK_EDGE, BLOCK_EDGE), (BLOCK_EDGE * DEVICE_SLOTS // 3) ** -0.5, 0.078125, ((0, 32),)),
        "probes": scatter_about(keys[1], (CELLS, PROBES), 1.0, 6.0, ((0, 32),)),
        "row_count": draw_row_count(jax.random.fold_in(keys[4], 71), 0),
        "column_of_slot": draw_column_of_slot(jax.random.fold_in(keys[4], 71), 0),
    }


def reference(blocks, probes, row_count, column_of_slot):
    omega = probes.reshape(CELLS // BLOCK_EDGE, BLOCK_EDGE, PROBES)
    stacked_blocks = blocks.reshape(DEVICES, DEVICE_SLOTS, BLOCK_EDGE, BLOCK_EDGE)
    column_list = column_of_slot.reshape(DEVICES, DEVICE_SLOTS)
    counts = row_count.reshape(DEVICES, RB)

    def one_device(items):
        block_set, column_set, count_set = items
        tiles = omega[column_set]
        prod = jnp.einsum("sij,sjk->sik", block_set.astype(jnp.float32), tiles.astype(jnp.float32))
        ends = jnp.cumsum(count_set).astype(jnp.int32)
        slot_entries = jnp.arange(DEVICE_SLOTS, dtype=jnp.int32)
        owner = jnp.sum((slot_entries[:, None] >= ends[None, :]).astype(jnp.int32), axis=1)
        onehot = (owner[None, :] == jnp.arange(RB, dtype=jnp.int32)[:, None]).astype(jnp.float32)
        summed = jnp.einsum("rs,sik->rik", onehot, prod, precision=lax.Precision.HIGHEST)
        return summed.reshape(RB * BLOCK_EDGE, PROBES)

    result = lax.map(one_device, (stacked_blocks, column_list, counts))
    return result.reshape(ROWS, PROBES)
```

```python
import functools

import jax
import jax.numpy as jnp
from jax import lax
from jax.experimental import pallas as pl
from jax.experimental.pallas import tpu as pltpu
from jax.sharding import PartitionSpec as P

STOPS = 4
LANES = 128


def kernel(geo, counts_ref, cols_ref, blocks_ref, probes_ref, out_ref,
           blk, win, inv_v, inv_s, recv, send, loc):
    loop_n, team_n, chunks, early, rows_here, slots, edge, tps = geo
    chunk = tps * edge // chunks
    per_piece = team_n * tps
    span = STOPS * per_piece
    t = lax.axis_index("loop")
    m = lax.axis_index("team")
    core = lax.rem(t, 2)

    def at(dt, dm):
        return {"loop": lax.rem(t + dt + loop_n, loop_n), "team": lax.rem(m + dm + team_n, team_n)}

    blk_copy = pltpu.make_async_copy(blocks_ref, blk.at[pl.ds(0, slots)], loc.at[0])
    blk_copy.start()
    own_copy = pltpu.make_async_copy(probes_ref, win.at[0, 0], loc.at[1])
    own_copy.start()

    barrier = pltpu.get_barrier_semaphore()
    peers = [(0, d) for d in range(1, team_n)]
    peers += [(1 - 2 * core, 0), (2, 0), (-2, 0), (6 * core - 3, 0)]
    for dt, dm in peers:
        pl.semaphore_signal(barrier, inc=1, device_id=at(dt, dm), device_id_type=pl.DeviceIdType.MESH)
    pl.semaphore_wait(barrier, len(peers))

    sent = []

    def rows(c):
        return pl.ds(c * chunk, chunk)

    def push(src, k, d, c, where, only=None):
        number = len(sent)
        copy = pltpu.make_async_remote_copy(
            src_ref=src, dst_ref=win.at[k, d, rows(c)],
            send_sem=send.at[number], recv_sem=recv.at[k, d, c],
            device_id=where, device_id_type=pl.DeviceIdType.MESH)
        sent.append((copy, only))
        if only is None:
            copy.start()
        else:
            pl.when(only)(copy.start)

    def arrive(k, d, c):
        pltpu.make_async_copy(win.at[k, d, rows(c)], win.at[k, d, rows(c)], recv.at[k, d, c]).wait()

    partner = at(1 - 2 * core, 0)
    across = at(1 + 2 * core, 0)
    lower = core == 0

    for c in range(chunks):
        own = probes_ref.at[rows(c)]
        for d in range(1, team_n):
            push(own, 0, d, c, at(0, d))
        push(own, 2, 0, c, at(2, 0))
        push(own, 1 + 2 * core, 0, c, across)

    place = lax.broadcasted_iota(jnp.int32, inv_v.shape, 0) * LANES
    place = place + lax.broadcasted_iota(jnp.int32, inv_v.shape, 1)

    def enter(s, table):
        col = cols_ref[s]
        stop = lax.rem(t - lax.div(col, per_piece) + loop_n, loop_n)
        within = lax.rem(col, per_piece)
        member = lax.rem(m - lax.div(within, tps) + team_n, team_n)
        key = (stop * team_n + member) * tps + lax.rem(within, tps)
        end = jnp.int32(0)
        for r in range(rows_here):
            end = end + counts_ref[r]
            key = key + jnp.where(s >= end, span, 0)
        return jnp.where((place == key) & (s < end), s, table)

    inv_v[...] = lax.fori_loop(0, slots, enter, jnp.full(inv_v.shape, slots, jnp.int32), unroll=4)
    inv_copy = pltpu.make_async_copy(inv_v, inv_s, loc.at[2])
    inv_copy.start()
    blk[slots] = jnp.zeros(blk.shape[1:], blk.dtype)
    out_ref[...] = jnp.zeros_like(out_ref)

    step = 2 if tps % 2 == 0 else 1

    def compute(k, d):
        base = (k * team_n + d) * tps
        total = None
        for j in range(0, tps, step):
            left = []
            for r in range(rows_here):
                pair = []
                for i in range(step):
                    key = r * span + base + j + i
                    pair.append(blk[inv_s[key // LANES, key % LANES]])
                left.append(jnp.concatenate(pair, axis=1))
            part = jnp.dot(jnp.concatenate(left, axis=0), win[k, d, pl.ds(j * edge, step * edge)],
                           preferred_element_type=jnp.float32)
            total = part if total is None else total + part
        out_ref[...] += total

    for c in range(chunks):
        for d in range(1, team_n):
            arrive(0, d, c)
            got = win.at[0, d, rows(c)]
            if c < early:
                push(got, 2, d, c, at(2, 0))
                push(got, 1 + 2 * core, d, c, across)
            else:
                push(got, 1, d, c, partner, lower)
        arrive(2, 0, c)
        got = win.at[2, 0, rows(c)]
        if c >= early:
            for d in range(1, team_n):
                push(got, 2, d, c, at(0, d))
        push(got, 3 - 2 * core, 0, c, partner)

    inv_copy.wait()
    blk_copy.wait()
    own_copy.wait()
    for d in range(team_n):
        compute(0, d)
    compute(2, 0)

    for c in range(chunks):
        arrive(3, 0, c)
        if c >= early:
            for d in range(1, team_n):
                push(win.at[3, 0, rows(c)], 3, d, c, at(0, d), lower)
        for d in range(1, team_n):
            arrive(2, d, c)
            push(win.at[2, d, rows(c)], 3 - 2 * core, d, c, partner)

    compute(3, 0)
    for d in range(1, team_n):
        compute(2, d)
    for d in range(team_n):
        for c in range(chunks):
            arrive(1, d, c)
        compute(1, d)
    for d in range(1, team_n):
        for c in range(chunks):
            arrive(3, d, c)
        compute(3, d)

    for copy, only in sent:
        if only is None:
            copy.wait_send()
        else:
            pl.when(only)(copy.wait_send)


def sends(team_n, chunks, early):
    late = chunks - early
    mates = team_n - 1
    return chunks * (mates + 2) + mates * (2 * early + late) + late * mates + chunks + late * mates + mates * chunks


def local(loop_n, team_n, blocks, probes, row_count, column_of_slot):
    slots, edge, _ = blocks.shape
    width = probes.shape[1]
    tps = probes.shape[0] // edge
    rows_here = row_count.shape[0]
    chunks = min(4, tps)
    early = chunks // 2
    geo = (loop_n, team_n, chunks, early, rows_here, slots, edge, tps)
    entries = rows_here * STOPS * team_n * tps
    table = (-(-entries // (8 * LANES)) * 8, LANES)
    return pl.pallas_call(
        functools.partial(kernel, geo),
        out_shape=jax.ShapeDtypeStruct((rows_here * edge, width), jnp.float32),
        in_specs=[
            pl.BlockSpec(memory_space=pltpu.SMEM),
            pl.BlockSpec(memory_space=pltpu.SMEM),
            pl.BlockSpec(memory_space=pltpu.HBM),
            pl.BlockSpec(memory_space=pltpu.HBM),
        ],
        out_specs=pl.BlockSpec(memory_space=pltpu.VMEM),
        scratch_shapes=[
            pltpu.VMEM((slots + 1, edge, edge), blocks.dtype),
            pltpu.VMEM((STOPS, team_n, tps * edge, width), probes.dtype),
            pltpu.VMEM(table, jnp.int32),
            pltpu.SMEM(table, jnp.int32),
            pltpu.SemaphoreType.DMA((STOPS, team_n, chunks)),
            pltpu.SemaphoreType.DMA((sends(team_n, chunks, early),)),
            pltpu.SemaphoreType.DMA((3,)),
        ],
        compiler_params=pltpu.CompilerParams(
            collective_id=0, has_side_effects=True, vmem_limit_bytes=60 * 1024 * 1024),
    )(row_count, column_of_slot, blocks, probes)


def solution(mesh):
    spec = ("loop", "team")
    return jax.shard_map(
        functools.partial(local, mesh.shape["loop"], mesh.shape["team"]),
        mesh=mesh,
        in_specs=(P(spec, None, None), P(spec, None), P(spec), P(spec)),
        out_specs=P(spec, None),
        check_vma=False,
    )
```

```python
import functools

import jax
import jax.numpy as jnp
from jax import lax
from jax.experimental import pallas as pl
from jax.experimental.pallas import tpu as pltpu
from jax.sharding import PartitionSpec as P

STOPS = 4
LANES = 128


def kernel(geo, counts_hbm, cols_hbm, blocks_ref, probes_ref, out_ref,
           blk, win, counts_ref, cols_ref, inv_v, inv_s, recv, send, loc):
    loop_n, team_n, chunks, early, early_wrap, rows_here, slots, edge, tps = geo
    chunk = tps * edge // chunks
    per_piece = team_n * tps
    span = STOPS * per_piece
    t = lax.axis_index("loop")
    m = lax.axis_index("team")
    core = lax.rem(t, 2)
    odd = lax.rem(lax.div(t, 2), 2)
    lower = core == 0
    passes = lower & (odd == 1)
    direct = (core == 0) | (odd == 0)

    def at(dt, dm):
        return {"loop": lax.rem(t + dt + loop_n, loop_n), "team": lax.rem(m + dm + team_n, team_n)}

    copies = [
        pltpu.make_async_copy(counts_hbm, counts_ref, loc.at[0]),
        pltpu.make_async_copy(cols_hbm, cols_ref, loc.at[1]),
        pltpu.make_async_copy(probes_ref, win.at[0, 0], loc.at[2]),
        pltpu.make_async_copy(blocks_ref, blk.at[pl.ds(0, slots)], loc.at[3]),
    ]
    for copy in copies:
        copy.start()

    barrier = pltpu.get_barrier_semaphore()

    def greet(dt, dm):
        pl.semaphore_signal(barrier, inc=1, device_id=at(dt, dm), device_id_type=pl.DeviceIdType.MESH)

    pl.when(lower)(lambda: greet(-3, 0))
    greet(jnp.where((core == 1) & (odd == 0), 1, -2), 0)
    for d in range(1, team_n):
        greet(0, d)
    greet(1 - 2 * core, 0)

    copies[0].wait()
    copies[1].wait()
    place = lax.broadcasted_iota(jnp.int32, inv_v.shape, 0) * LANES
    place = place + lax.broadcasted_iota(jnp.int32, inv_v.shape, 1)

    def enter(s, table):
        col = cols_ref[s]
        stop = lax.rem(t - lax.div(col, per_piece) + loop_n, loop_n)
        within = lax.rem(col, per_piece)
        member = lax.rem(m - lax.div(within, tps) + team_n, team_n)
        key = (stop * team_n + member) * tps + lax.rem(within, tps)
        end = jnp.int32(0)
        for r in range(rows_here):
            end = end + counts_ref[r]
            key = key + jnp.where(s >= end, span, 0)
        return jnp.where((place == key) & (s < end), s, table)

    inv_v[...] = lax.fori_loop(0, slots, enter, jnp.full(inv_v.shape, slots, jnp.int32), unroll=8)
    inv_copy = pltpu.make_async_copy(inv_v, inv_s, loc.at[4])
    inv_copy.start()
    blk[slots] = jnp.zeros(blk.shape[1:], blk.dtype)

    pl.semaphore_wait(barrier, team_n + 1 + jnp.where(core == odd, 0, 1))

    sent = []

    def rows(c):
        return pl.ds(c * chunk, chunk)

    def push(src, k, d, c, where, only=None):
        copy = pltpu.make_async_remote_copy(
            src_ref=src, dst_ref=win.at[k, d, rows(c)],
            send_sem=send.at[len(sent)], recv_sem=recv.at[k, d, c],
            device_id=where, device_id_type=pl.DeviceIdType.MESH)
        sent.append((copy, only))
        if only is None:
            copy.start()
        else:
            pl.when(only)(copy.start)

    def arrive(k, d, c):
        pltpu.make_async_copy(win.at[k, d, rows(c)], win.at[k, d, rows(c)], recv.at[k, d, c]).wait()

    def first(c, limit):
        return limit > c

    partner = at(1 - 2 * core, 0)
    ahead = at(2, 0)
    across = at(1 + 2 * core, 0)
    back = at(-1, 0)
    out2 = jnp.where(t + 2 >= loop_n, early_wrap, early)
    out3 = jnp.where(t + 3 >= loop_n, early_wrap, early)
    in2 = jnp.where(t < 2, early_wrap, early)
    in3 = jnp.where(t < 3, early_wrap, early)

    for c in range(chunks):
        own = probes_ref.at[rows(c)]
        for d in range(1, team_n):
            push(own, 0, d, c, at(0, d))
        push(own, 1 + 2 * core, 0, c, across)
        push(own, 2, 0, c, ahead, direct)

    inv_copy.wait()
    copies[2].wait()
    copies[3].wait()
    step = 2 if tps % 2 == 0 else 1

    def compute(k, d):
        base = (k * team_n + d) * tps
        total = None
        for j in range(0, tps, step):
            left = []
            for r in range(rows_here):
                pair = []
                for i in range(step):
                    key = r * span + base + j + i
                    pair.append(blk[inv_s[key // LANES, key % LANES]])
                left.append(jnp.concatenate(pair, axis=1))
            part = jnp.dot(jnp.concatenate(left, axis=0), win[k, d, pl.ds(j * edge, step * edge)],
                           preferred_element_type=jnp.float32)
            total = part if total is None else total + part
        if k == 0 and d == 0:
            out_ref[...] = total
        else:
            out_ref[...] += total

    compute(0, 0)
    for c in range(chunks):
        for d in range(1, team_n):
            arrive(0, d, c)
            got = win.at[0, d, rows(c)]
            push(got, 2, d, c, ahead, direct & first(c, out2))
            push(got, 1 + 2 * core, d, c, across, lower | first(c, out3))
    for d in range(1, team_n):
        compute(0, d)

    for c in range(chunks):
        @pl.when(lower)
        def _():
            arrive(3, 0, c)
        got = win.at[3, 0, rows(c)]
        push(got, 2, 0, c, back, passes)
        for d in range(1, team_n):
            push(got, 3, d, c, at(0, d), lower & ~first(c, in3))
        arrive(2, 0, c)
        got = win.at[2, 0, rows(c)]
        for d in range(1, team_n):
            push(got, 2, d, c, at(0, d), ~first(c, in2))
        push(got, 3 - 2 * core, 0, c, partner)
    compute(2, 0)

    for c in range(chunks):
        for d in range(1, team_n):
            @pl.when(lower)
            def _():
                arrive(3, d, c)
            push(win.at[3, d, rows(c)], 2, d, c, back, passes & first(c, in3))
            arrive(2, d, c)
            push(win.at[2, d, rows(c)], 3 - 2 * core, d, c, partner)

    for d in range(1, team_n):
        compute(2, d)
    for d in range(team_n):
        for c in range(chunks):
            arrive(1, d, c)
        compute(1, d)
    for d in range(team_n):
        @pl.when(core == 1)
        def _():
            for c in range(chunks):
                arrive(3, d, c)
        compute(3, d)

    for copy, only in sent:
        if only is None:
            copy.wait_send()
        else:
            pl.when(only)(copy.wait_send)


def sends(team_n, chunks):
    mates = team_n - 1
    return chunks * (mates + 2 + 2 * mates + 1 + mates + mates + 1 + 2 * mates)


def local(loop_n, team_n, blocks, probes, row_count, column_of_slot):
    slots, edge, _ = blocks.shape
    width = probes.shape[1]
    tps = probes.shape[0] // edge
    rows_here = row_count.shape[0]
    chunks = min(8, tps)
    early = chunks * 5 // 8
    early_wrap = chunks // 4
    geo = (loop_n, team_n, chunks, early, early_wrap, rows_here, slots, edge, tps)
    entries = rows_here * STOPS * team_n * tps
    table = (-(-entries // (8 * LANES)) * 8, LANES)
    return pl.pallas_call(
        functools.partial(kernel, geo),
        out_shape=jax.ShapeDtypeStruct((rows_here * edge, width), jnp.float32),
        in_specs=[
            pl.BlockSpec(memory_space=pltpu.HBM),
            pl.BlockSpec(memory_space=pltpu.HBM),
            pl.BlockSpec(memory_space=pltpu.HBM),
            pl.BlockSpec(memory_space=pltpu.HBM),
        ],
        out_specs=pl.BlockSpec(memory_space=pltpu.VMEM),
        scratch_shapes=[
            pltpu.VMEM((slots + 1, edge, edge), blocks.dtype),
            pltpu.VMEM((STOPS, team_n, tps * edge, width), probes.dtype),
            pltpu.SMEM(row_count.shape, jnp.int32),
            pltpu.SMEM(column_of_slot.shape, jnp.int32),
            pltpu.VMEM(table, jnp.int32),
            pltpu.SMEM(table, jnp.int32),
            pltpu.SemaphoreType.DMA((STOPS, team_n, chunks)),
            pltpu.SemaphoreType.DMA((sends(team_n, chunks),)),
            pltpu.SemaphoreType.DMA((5,)),
        ],
        compiler_params=pltpu.CompilerParams(
            collective_id=0, has_side_effects=True, vmem_limit_bytes=60 * 1024 * 1024),
    )(row_count, column_of_slot, blocks, probes)


def solution(mesh):
    spec = ("loop", "team")
    return jax.shard_map(
        functools.partial(local, mesh.shape["loop"], mesh.shape["team"]),
        mesh=mesh,
        in_specs=(P(spec, None, None), P(spec, None), P(spec), P(spec)),
        out_specs=P(spec, None),
        check_vma=False,
    )
```

```python
import functools

import jax
import jax.numpy as jnp
from jax import lax
from jax.experimental import pallas as pl
from jax.experimental.pallas import tpu as pltpu
from jax.sharding import PartitionSpec as P

STOPS = 4
LANES = 128


def div(x, n):
    return lax.shift_right_logical(x, n.bit_length() - 1) if n & (n - 1) == 0 else lax.div(x, n)


def rem(x, n):
    return x & (n - 1) if n & (n - 1) == 0 else lax.rem(x, n)


def kernel(geo, counts_hbm, cols_hbm, blocks_ref, probes_ref, out_ref,
           blk, win, counts_ref, cols_ref, inv_v, inv_s, recv, send, loc):
    loop_n, team_n, chunks, early, rows_here, slots, edge, tps = geo
    chunk = tps * edge // chunks
    per_piece = team_n * tps
    span = STOPS * per_piece
    t = lax.axis_index("loop")
    m = lax.axis_index("team")
    core = lax.rem(t, 2)
    odd = lax.rem(lax.div(t, 2), 2)
    lower = core == 0

    def at(dt, dm):
        return {"loop": lax.rem(t + dt + loop_n, loop_n), "team": lax.rem(m + dm + team_n, team_n)}

    copies = [
        pltpu.make_async_copy(counts_hbm, counts_ref, loc.at[0]),
        pltpu.make_async_copy(cols_hbm, cols_ref, loc.at[1]),
        pltpu.make_async_copy(probes_ref, win.at[0, 0], loc.at[2]),
        pltpu.make_async_copy(blocks_ref, blk.at[pl.ds(0, slots)], loc.at[3]),
    ]
    for copy in copies:
        copy.start()

    barrier = pltpu.get_barrier_semaphore()

    def greet(dt, dm):
        pl.semaphore_signal(barrier, inc=1, device_id=at(dt, dm), device_id_type=pl.DeviceIdType.MESH)

    pl.when(lower)(lambda: greet(-3, 0))
    greet(-2, 0)
    for d in range(1, team_n):
        greet(0, d)
    greet(1 - 2 * core, 0)

    copies[0].wait()
    copies[1].wait()
    col = cols_ref[...]
    within = rem(col, per_piece)
    stop = rem(t - div(col, per_piece) + loop_n, loop_n)
    member = rem(m - div(within, tps) + team_n, team_n)
    key = (stop * team_n + member) * tps + rem(within, tps)
    number = lax.broadcasted_iota(jnp.int32, key.shape, 1)
    end = jnp.int32(0)
    for r in range(rows_here):
        end = end + counts_ref[r]
        key = key + jnp.where(number >= end, span, 0)
    key = jnp.where(number < end, key, -1)
    entries = inv_v.shape[1]
    keys = jnp.broadcast_to(key, (LANES, slots)).T[:, :1]
    hit = keys == lax.broadcasted_iota(jnp.int32, (slots, entries), 1)
    owner = jnp.where(hit, lax.broadcasted_iota(jnp.int32, (slots, entries), 0), slots)
    inv_v[...] = jnp.min(owner, axis=0, keepdims=True)
    inv_copy = pltpu.make_async_copy(inv_v, inv_s, loc.at[4])
    inv_copy.start()
    blk[slots] = jnp.zeros(blk.shape[1:], blk.dtype)

    pl.semaphore_wait(barrier, team_n + 1 + core)

    sent = []

    def rows(c):
        return pl.ds(c * chunk, chunk)

    def push(src, k, d, c, where, only=None):
        copy = pltpu.make_async_remote_copy(
            src_ref=src, dst_ref=win.at[k, d, rows(c)],
            send_sem=send.at[len(sent)], recv_sem=recv.at[k, d, c],
            device_id=where, device_id_type=pl.DeviceIdType.MESH)
        sent.append((copy, only))
        if only is None:
            copy.start()
        else:
            pl.when(only)(copy.start)

    def arrive(k, d, c):
        pltpu.make_async_copy(win.at[k, d, rows(c)], win.at[k, d, rows(c)], recv.at[k, d, c]).wait()

    def first(c, limit):
        return limit > c

    partner = at(1 - 2 * core, 0)
    ahead = at(2, 0)
    across = at(1 + 2 * core, 0)
    even2, odd2, even3, odd3 = early
    out2 = jnp.where(odd == 1, odd2, even2)
    out3 = jnp.where(odd == 1, odd3, even3)
    in2 = jnp.where(odd == 1, even2, odd2)
    in3 = out3

    for c in range(chunks):
        own = probes_ref.at[rows(c)]
        push(own, 2, 0, c, ahead)
        push(own, 1 + 2 * core, 0, c, across)
        for d in range(1, team_n):
            push(own, 0, d, c, at(0, d))

    inv_copy.wait()
    copies[2].wait()
    copies[3].wait()
    step = 2 if tps % 2 == 0 else 1

    def compute(k, d):
        base = (k * team_n + d) * tps
        total = None
        for j in range(0, tps, step):
            left = []
            for r in range(rows_here):
                pair = []
                for i in range(step):
                    key = r * span + base + j + i
                    pair.append(blk[inv_s[0, key]])
                left.append(jnp.concatenate(pair, axis=1))
            part = jnp.dot(jnp.concatenate(left, axis=0), win[k, d, pl.ds(j * edge, step * edge)],
                           preferred_element_type=jnp.float32)
            total = part if total is None else total + part
        if k == 0 and d == 0:
            out_ref[...] = total
        else:
            out_ref[...] += total

    compute(0, 0)
    for c in range(chunks):
        for d in range(1, team_n):
            arrive(0, d, c)
            got = win.at[0, d, rows(c)]
            push(got, 2, d, c, ahead, first(c, out2))
            push(got, 1 + 2 * core, d, c, across, lower | first(c, out3))

    for c in range(chunks):
        arrive(2, 0, c)
        got = win.at[2, 0, rows(c)]
        for d in range(1, team_n):
            push(got, 2, d, c, at(0, d), ~first(c, in2))
        push(got, 3 - 2 * core, 0, c, partner)

        @pl.when(lower)
        def _():
            arrive(3, 0, c)
        for d in range(1, team_n):
            push(win.at[3, 0, rows(c)], 3, d, c, at(0, d), lower & ~first(c, in3))

    for d in range(1, team_n):
        compute(0, d)
    compute(2, 0)
    for c in range(chunks):
        arrive(1, 0, c)
    compute(1, 0)

    @pl.when(core == 1)
    def _():
        for c in range(chunks):
            arrive(3, 0, c)
    compute(3, 0)

    for c in range(chunks):
        for d in range(1, team_n):
            arrive(2, d, c)
            push(win.at[2, d, rows(c)], 3 - 2 * core, d, c, partner)

    for k in (2, 1, 3):
        for d in range(1, team_n):
            if k != 2:
                for c in range(chunks):
                    arrive(k, d, c)
            compute(k, d)

    for copy, only in sent:
        if only is None:
            copy.wait_send()
        else:
            pl.when(only)(copy.wait_send)


def sends(team_n, chunks):
    mates = team_n - 1
    return chunks * (2 + mates + 2 * mates + mates + 1 + mates + mates)


def local(loop_n, team_n, blocks, probes, row_count, column_of_slot):
    slots, edge, _ = blocks.shape
    width = probes.shape[1]
    tps = probes.shape[0] // edge
    rows_here = row_count.shape[0]
    chunks = min(4, tps)
    early = (chunks // 2, chunks // 4, chunks, chunks // 4)
    geo = (loop_n, team_n, chunks, early, rows_here, slots, edge, tps)
    entries = rows_here * STOPS * team_n * tps
    table = (1, -(-entries // LANES) * LANES)
    return pl.pallas_call(
        functools.partial(kernel, geo),
        out_shape=jax.ShapeDtypeStruct((rows_here * edge, width), jnp.float32),
        in_specs=[
            pl.BlockSpec(memory_space=pltpu.HBM),
            pl.BlockSpec(memory_space=pltpu.HBM),
            pl.BlockSpec(memory_space=pltpu.HBM),
            pl.BlockSpec(memory_space=pltpu.HBM),
        ],
        out_specs=pl.BlockSpec(memory_space=pltpu.VMEM),
        scratch_shapes=[
            pltpu.VMEM((slots + 1, edge, edge), blocks.dtype),
            pltpu.VMEM((STOPS, team_n, tps * edge, width), probes.dtype),
            pltpu.SMEM(row_count.shape, jnp.int32),
            pltpu.VMEM((1, slots), jnp.int32),
            pltpu.VMEM(table, jnp.int32),
            pltpu.SMEM(table, jnp.int32),
            pltpu.SemaphoreType.DMA((STOPS, team_n, chunks)),
            pltpu.SemaphoreType.DMA((sends(team_n, chunks),)),
            pltpu.SemaphoreType.DMA((5,)),
        ],
        compiler_params=pltpu.CompilerParams(
            collective_id=0, has_side_effects=True, vmem_limit_bytes=60 * 1024 * 1024),
    )(row_count, column_of_slot.reshape(1, slots), blocks, probes)


def solution(mesh):
    spec = ("loop", "team")
    return jax.shard_map(
        functools.partial(local, mesh.shape["loop"], mesh.shape["team"]),
        mesh=mesh,
        in_specs=(P(spec, None, None), P(spec, None), P(spec), P(spec)),
        out_specs=P(spec, None),
        check_vma=False,
    )
```

```python
import functools

import jax
import jax.numpy as jnp
from jax import lax
from jax.experimental import pallas as pl
from jax.experimental.pallas import tpu as pltpu
from jax.sharding import PartitionSpec as P

STOPS = 4
LANES = 128


def div(x, n):
    return lax.shift_right_logical(x, n.bit_length() - 1) if n & (n - 1) == 0 else lax.div(x, n)


def rem(x, n):
    return x & (n - 1) if n & (n - 1) == 0 else lax.rem(x, n)


def kernel(geo, meta_ref, blocks_ref, probes_ref, out_ref,
           blk, win, inv_v, inv_s, recv, send, loc):
    loop_n, team_n, chunks, early, rows_here, slots, edge, tps = geo
    chunk = tps * edge // chunks
    per_piece = team_n * tps
    span = STOPS * per_piece
    t = lax.axis_index("loop")
    m = lax.axis_index("team")
    core = lax.rem(t, 2)
    odd = lax.rem(lax.div(t, 2), 2)
    lower = core == 0

    def at(dt, dm):
        return {"loop": lax.rem(t + dt + loop_n, loop_n), "team": lax.rem(m + dm + team_n, team_n)}

    copies = [
        pltpu.make_async_copy(probes_ref, win.at[0, 0], loc.at[0]),
        pltpu.make_async_copy(blocks_ref, blk.at[pl.ds(0, slots)], loc.at[1]),
    ]

    barrier = pltpu.get_barrier_semaphore()

    def greet(dt, dm):
        pl.semaphore_signal(barrier, inc=1, device_id=at(dt, dm), device_id_type=pl.DeviceIdType.MESH)

    pl.when(lower)(lambda: greet(-3, 0))
    greet(-2, 0)
    for d in range(1, team_n):
        greet(0, d)
    greet(1 - 2 * core, 0)

    for copy in copies:
        copy.start()

    col = meta_ref[:, :slots]
    within = rem(col, per_piece)
    stop = rem(t - div(col, per_piece) + loop_n, loop_n)
    member = rem(m - div(within, tps) + team_n, team_n)
    key = (stop * team_n + member) * tps + rem(within, tps)
    number = lax.broadcasted_iota(jnp.int32, key.shape, 1)
    end = jnp.zeros((1, 1), jnp.int32)
    for r in range(rows_here):
        end = end + meta_ref[:, slots + r:slots + r + 1]
        key = key + jnp.where(number >= end, span, 0)
    key = jnp.where(number < end, key, -1)
    entries = inv_v.shape[1]
    keys = jnp.broadcast_to(key, (LANES, slots)).T[:, :1]
    hit = keys == lax.broadcasted_iota(jnp.int32, (slots, entries), 1)
    owner = jnp.where(hit, lax.broadcasted_iota(jnp.int32, (slots, entries), 0), slots)
    inv_v[...] = jnp.min(owner, axis=0, keepdims=True)
    inv_copy = pltpu.make_async_copy(inv_v, inv_s, loc.at[2])
    inv_copy.start()
    blk[slots] = jnp.zeros(blk.shape[1:], blk.dtype)

    pl.semaphore_wait(barrier, team_n + 1 + core)

    sent = []

    def rows(c):
        return pl.ds(c * chunk, chunk)

    def push(src, k, d, c, where, only=None):
        copy = pltpu.make_async_remote_copy(
            src_ref=src, dst_ref=win.at[k, d, rows(c)],
            send_sem=send.at[len(sent)], recv_sem=recv.at[k, d, c],
            device_id=where, device_id_type=pl.DeviceIdType.MESH)
        sent.append((copy, only))
        if only is None:
            copy.start()
        else:
            pl.when(only)(copy.start)

    def arrive(k, d, c):
        pltpu.make_async_copy(win.at[k, d, rows(c)], win.at[k, d, rows(c)], recv.at[k, d, c]).wait()

    def first(c, limit):
        return limit > c

    partner = at(1 - 2 * core, 0)
    ahead = at(2, 0)
    across = at(1 + 2 * core, 0)
    even2, odd2, even3, odd3 = early
    out2 = jnp.where(odd == 1, odd2, even2)
    out3 = jnp.where(odd == 1, odd3, even3)
    in2 = jnp.where(odd == 1, even2, odd2)
    in3 = out3
    out2 = jnp.where(t + 2 >= loop_n, 0, out2)
    out3 = jnp.where((t + 3 >= loop_n) & (odd == 1), 0, out3)
    in2 = jnp.where(t < 2, 0, in2)
    in3 = jnp.where((t < 3) & (odd == 1), 0, in3)

    for c in range(chunks):
        own = probes_ref.at[rows(c)]
        push(own, 2, 0, c, ahead)
        push(own, 1 + 2 * core, 0, c, across)
        for d in range(1, team_n):
            push(own, 0, d, c, at(0, d))

    inv_copy.wait()
    for copy in copies:
        copy.wait()
    step = 2 if tps % 2 == 0 else 1

    def compute(k, d):
        base = (k * team_n + d) * tps
        total = None
        for j in range(0, tps, step):
            left = []
            for r in range(rows_here):
                pair = []
                for i in range(step):
                    key = r * span + base + j + i
                    pair.append(blk[inv_s[0, key]])
                left.append(jnp.concatenate(pair, axis=1))
            part = jnp.dot(jnp.concatenate(left, axis=0), win[k, d, pl.ds(j * edge, step * edge)],
                           preferred_element_type=jnp.float32)
            total = part if total is None else total + part
        if k == 0 and d == 0:
            out_ref[...] = total
        else:
            out_ref[...] += total

    compute(0, 0)
    for c in range(chunks):
        for d in range(1, team_n):
            arrive(0, d, c)
            got = win.at[0, d, rows(c)]
            push(got, 2, d, c, ahead, first(c, out2))
            push(got, 1 + 2 * core, d, c, across, lower | first(c, out3))

    for c in range(chunks):
        arrive(2, 0, c)
        got = win.at[2, 0, rows(c)]
        for d in range(1, team_n):
            push(got, 2, d, c, at(0, d), ~first(c, in2))
        push(got, 3 - 2 * core, 0, c, partner)

        @pl.when(lower)
        def _():
            arrive(3, 0, c)
        for d in range(1, team_n):
            push(win.at[3, 0, rows(c)], 3, d, c, at(0, d), lower & ~first(c, in3))

    for d in range(1, team_n):
        compute(0, d)
    compute(2, 0)
    for c in range(chunks):
        arrive(1, 0, c)
    compute(1, 0)

    @pl.when(core == 1)
    def _():
        for c in range(chunks):
            arrive(3, 0, c)
    compute(3, 0)

    for c in range(chunks):
        for d in range(1, team_n):
            arrive(2, d, c)
            push(win.at[2, d, rows(c)], 3 - 2 * core, d, c, partner)

    for k in (2, 1, 3):
        for d in range(1, team_n):
            if k != 2:
                for c in range(chunks):
                    arrive(k, d, c)
            compute(k, d)

    for copy, only in sent:
        if only is None:
            copy.wait_send()
        else:
            pl.when(only)(copy.wait_send)


def sends(team_n, chunks):
    mates = team_n - 1
    return chunks * (2 + mates + 2 * mates + mates + 1 + mates + mates)


def local(loop_n, team_n, blocks, probes, row_count, column_of_slot):
    slots, edge, _ = blocks.shape
    width = probes.shape[1]
    tps = probes.shape[0] // edge
    rows_here = row_count.shape[0]
    chunks = min(4, tps)
    early = (chunks // 2, chunks // 4, chunks, chunks // 4)
    geo = (loop_n, team_n, chunks, early, rows_here, slots, edge, tps)
    entries = rows_here * STOPS * team_n * tps
    table = (1, -(-entries // LANES) * LANES)
    meta = jnp.concatenate([column_of_slot, row_count]).reshape(1, slots + rows_here)
    return pl.pallas_call(
        functools.partial(kernel, geo),
        out_shape=jax.ShapeDtypeStruct((rows_here * edge, width), jnp.float32),
        in_specs=[
            pl.BlockSpec(memory_space=pltpu.VMEM),
            pl.BlockSpec(memory_space=pltpu.HBM),
            pl.BlockSpec(memory_space=pltpu.HBM),
        ],
        out_specs=pl.BlockSpec(memory_space=pltpu.VMEM),
        scratch_shapes=[
            pltpu.VMEM((slots + 1, edge, edge), blocks.dtype),
            pltpu.VMEM((STOPS, team_n, tps * edge, width), probes.dtype),
            pltpu.VMEM(table, jnp.int32),
            pltpu.SMEM(table, jnp.int32),
            pltpu.SemaphoreType.DMA((STOPS, team_n, chunks)),
            pltpu.SemaphoreType.DMA((sends(team_n, chunks),)),
            pltpu.SemaphoreType.DMA((3,)),
        ],
        compiler_params=pltpu.CompilerParams(
            collective_id=0, has_side_effects=True, vmem_limit_bytes=55000 * 1024),
    )(meta, blocks, probes)


def solution(mesh):
    spec = ("loop", "team")
    return jax.shard_map(
        functools.partial(local, mesh.shape["loop"], mesh.shape["team"]),
        mesh=mesh,
        in_specs=(P(spec, None, None), P(spec, None), P(spec), P(spec)),
        out_specs=P(spec, None),
        check_vma=False,
    )
```

```python
import functools

import jax
import jax.numpy as jnp
from jax import lax
from jax.experimental import pallas as pl
from jax.experimental.pallas import tpu as pltpu
from jax.sharding import PartitionSpec as P

STOPS = 4
LANES = 128


def div(x, n):
    return lax.shift_right_logical(x, n.bit_length() - 1) if n & (n - 1) == 0 else lax.div(x, n)


def rem(x, n):
    return x & (n - 1) if n & (n - 1) == 0 else lax.rem(x, n)


def kernel(geo, meta_ref, blocks_ref, probes_ref, out_ref,
           blk, win, inv_v, inv_s, recv, send, loc):
    loop_n, team_n, chunks, early, rows_here, slots, edge, tps = geo
    chunk = tps * edge // chunks
    per_piece = team_n * tps
    span = STOPS * per_piece
    t = lax.axis_index("loop")
    m = lax.axis_index("team")
    core = lax.rem(t, 2)
    odd = lax.rem(lax.div(t, 2), 2)
    lower = core == 0

    def at(dt, dm):
        return {"loop": lax.rem(t + dt + loop_n, loop_n), "team": lax.rem(m + dm + team_n, team_n)}

    copies = [
        pltpu.make_async_copy(probes_ref, win.at[0, 0], loc.at[0]),
        pltpu.make_async_copy(blocks_ref, blk.at[pl.ds(0, slots)], loc.at[1]),
    ]

    barrier = pltpu.get_barrier_semaphore()

    def greet(dt, dm):
        pl.semaphore_signal(barrier, inc=1, device_id=at(dt, dm), device_id_type=pl.DeviceIdType.MESH)

    pl.when(lower)(lambda: greet(-3, 0))
    greet(jnp.where(t == 1, 1, -2), 0)
    for d in range(1, team_n):
        greet(0, d)
    greet(1 - 2 * core, 0)

    for copy in copies:
        copy.start()

    col = meta_ref[:, :slots]
    within = rem(col, per_piece)
    stop = rem(t - div(col, per_piece) + loop_n, loop_n)
    member = rem(m - div(within, tps) + team_n, team_n)
    key = (stop * team_n + member) * tps + rem(within, tps)
    number = lax.broadcasted_iota(jnp.int32, key.shape, 1)
    end = jnp.zeros((1, 1), jnp.int32)
    for r in range(rows_here):
        end = end + meta_ref[:, slots + r:slots + r + 1]
        key = key + jnp.where(number >= end, span, 0)
    key = jnp.where(number < end, key, -1)
    entries = inv_v.shape[1]
    keys = jnp.broadcast_to(key, (LANES, slots)).T[:, :1]
    hit = keys == lax.broadcasted_iota(jnp.int32, (slots, entries), 1)
    owner = jnp.where(hit, lax.broadcasted_iota(jnp.int32, (slots, entries), 0), slots)
    inv_v[...] = jnp.min(owner, axis=0, keepdims=True)
    inv_copy = pltpu.make_async_copy(inv_v, inv_s, loc.at[2])
    inv_copy.start()
    blk[slots] = jnp.zeros(blk.shape[1:], blk.dtype)

    pl.semaphore_wait(barrier, team_n + 1 + core + jnp.where(t == 2, 1, 0) - jnp.where(t == loop_n - 1, 1, 0))

    sent = []

    def rows(c):
        return pl.ds(c * chunk, chunk)

    def push(src, k, d, c, where, only=None):
        copy = pltpu.make_async_remote_copy(
            src_ref=src, dst_ref=win.at[k, d, rows(c)],
            send_sem=send.at[len(sent)], recv_sem=recv.at[k, d, c],
            device_id=where, device_id_type=pl.DeviceIdType.MESH)
        sent.append((copy, only))
        if only is None:
            copy.start()
        else:
            pl.when(only)(copy.start)

    def arrive(k, d, c):
        pltpu.make_async_copy(win.at[k, d, rows(c)], win.at[k, d, rows(c)], recv.at[k, d, c]).wait()

    def first(c, limit):
        return limit > c

    partner = at(1 - 2 * core, 0)
    ahead = at(2, 0)
    across = at(1 + 2 * core, 0)
    even2, odd2, even3, odd3 = early
    out2 = jnp.where(odd == 1, odd2, even2)
    out3 = jnp.where(odd == 1, odd3, even3)
    in2 = jnp.where(odd == 1, even2, odd2)
    in3 = out3
    out2 = jnp.where(t + 2 >= loop_n, 0, out2)
    out3 = jnp.where((t + 3 >= loop_n) & (odd == 1), 0, out3)
    in2 = jnp.where(t < 2, 0, in2)
    in3 = jnp.where((t < 3) & (odd == 1), 0, in3)

    for c in range(chunks):
        own = probes_ref.at[rows(c)]
        push(own, 2, 0, c, ahead, t != loop_n - 1)
        push(own, 1 + 2 * core, 0, c, across)
        for d in range(1, team_n):
            push(own, 0, d, c, at(0, d))

    inv_copy.wait()
    for copy in copies:
        copy.wait()
    step = 2 if tps % 2 == 0 else 1

    def compute(k, d):
        base = (k * team_n + d) * tps
        total = None
        for j in range(0, tps, step):
            left = []
            for r in range(rows_here):
                pair = []
                for i in range(step):
                    key = r * span + base + j + i
                    pair.append(blk[inv_s[0, key]])
                left.append(jnp.concatenate(pair, axis=1))
            part = jnp.dot(jnp.concatenate(left, axis=0), win[k, d, pl.ds(j * edge, step * edge)],
                           preferred_element_type=jnp.float32)
            total = part if total is None else total + part
        if k == 0 and d == 0:
            out_ref[...] = total
        else:
            out_ref[...] += total

    compute(0, 0)
    for c in range(chunks):
        for d in range(1, team_n):
            arrive(0, d, c)
            got = win.at[0, d, rows(c)]
            push(got, 2, d, c, ahead, first(c, out2))
            push(got, 1 + 2 * core, d, c, across, lower | first(c, out3))

    for c in range(chunks):
        arrive(2, 0, c)
        got = win.at[2, 0, rows(c)]
        for d in range(1, team_n):
            push(got, 2, d, c, at(0, d), ~first(c, in2))
        push(got, 3 - 2 * core, 0, c, partner)

        @pl.when(lower)
        def _():
            arrive(3, 0, c)
        push(win.at[3, 0, rows(c)], 2, 0, c, at(-1, 0), t == 2)
        for d in range(1, team_n):
            push(win.at[3, 0, rows(c)], 3, d, c, at(0, d), lower & ~first(c, in3))

    for d in range(1, team_n):
        compute(0, d)
    compute(2, 0)
    for c in range(chunks):
        arrive(1, 0, c)
    compute(1, 0)

    @pl.when(core == 1)
    def _():
        for c in range(chunks):
            arrive(3, 0, c)
    compute(3, 0)

    for c in range(chunks):
        for d in range(1, team_n):
            arrive(2, d, c)
            push(win.at[2, d, rows(c)], 3 - 2 * core, d, c, partner)

    for k in (2, 1, 3):
        for d in range(1, team_n):
            if k != 2:
                for c in range(chunks):
                    arrive(k, d, c)
            compute(k, d)

    for copy, only in sent:
        if only is None:
            copy.wait_send()
        else:
            pl.when(only)(copy.wait_send)


def sends(team_n, chunks):
    mates = team_n - 1
    return chunks * (2 + mates + 2 * mates + mates + 1 + mates + mates + 1)


def local(loop_n, team_n, blocks, probes, row_count, column_of_slot):
    slots, edge, _ = blocks.shape
    width = probes.shape[1]
    tps = probes.shape[0] // edge
    rows_here = row_count.shape[0]
    chunks = min(4, tps)
    early = (chunks // 2, chunks // 4, chunks, chunks // 4)
    geo = (loop_n, team_n, chunks, early, rows_here, slots, edge, tps)
    entries = rows_here * STOPS * team_n * tps
    table = (1, -(-entries // LANES) * LANES)
    meta = jnp.concatenate([column_of_slot, row_count]).reshape(1, slots + rows_here)
    return pl.pallas_call(
        functools.partial(kernel, geo),
        out_shape=jax.ShapeDtypeStruct((rows_here * edge, width), jnp.float32),
        in_specs=[
            pl.BlockSpec(memory_space=pltpu.VMEM),
            pl.BlockSpec(memory_space=pltpu.HBM),
            pl.BlockSpec(memory_space=pltpu.HBM),
        ],
        out_specs=pl.BlockSpec(memory_space=pltpu.VMEM),
        scratch_shapes=[
            pltpu.VMEM((slots + 1, edge, edge), blocks.dtype),
            pltpu.VMEM((STOPS, team_n, tps * edge, width), probes.dtype),
            pltpu.VMEM(table, jnp.int32),
            pltpu.SMEM(table, jnp.int32),
            pltpu.SemaphoreType.DMA((STOPS, team_n, chunks)),
            pltpu.SemaphoreType.DMA((sends(team_n, chunks),)),
            pltpu.SemaphoreType.DMA((3,)),
        ],
        compiler_params=pltpu.CompilerParams(
            collective_id=0, has_side_effects=True, vmem_limit_bytes=55000 * 1024),
    )(meta, blocks, probes)


def solution(mesh):
    spec = ("loop", "team")
    return jax.shard_map(
        functools.partial(local, mesh.shape["loop"], mesh.shape["team"]),
        mesh=mesh,
        in_specs=(P(spec, None, None), P(spec, None), P(spec), P(spec)),
        out_specs=P(spec, None),
        check_vma=False,
    )
```
